32 devices in a mesh: groups: 2 (over x), track: 4 (over y, core), frame: 4 (over z).
Axes of the slice: x: 2, y: 2, z: 4, core: 2. Of those that a mesh axis runs over, the one named last changes fastest.
Arguments:
- frames: bfloat16 [16, 4096, 256], P(('groups', 'frame')), parts along dimension 0, may hold values from -9 to 9
- query_frame: int32 [1024], P(('groups', 'track')), parts along dimension 0, may hold values from 0 to 7
- query_pixel: int32 [1024], P(('groups', 'track')), parts along dimension 0, may hold values from 0 to 4095
- cotangent: float32 [2, 16, 512], P(None, ('groups', 'frame'), 'track'), parts along dimension 1, may hold values from -48 to 48
Outputs:
- frame_grad: float32 [4096, 16, 256], P('track', ('groups', 'frame')), parts along dimension 1
- query_grad: float32 [1024, 256], P(('groups', 'track', 'frame')), parts along dimension 0
The draws below stay inside these ranges and needn't reach their ends.
There are 2 independent parts, one for each index of `groups`. The reference program is written for one: setup_inputs(seed, part) draws one part's arguments, and reference() takes and returns one part's arrays. A program takes and returns all parts, laid end to end along the dimension named above; each array names one. Nothing has to cross between parts.
All inputs are finite; a program needn't handle non-finite values.
Results may differ from the reference program's by a relative error of at most 0.0029.
Values may be sent and summed in bfloat16 or wider, within the bound.
No kernel may reach another device: no remote copies, remote signals or barrier semaphores. Data moves between devices by JAX's collectives and lax.ppermute only.
A program may use at most 64 MiB of HBM per device.

```python
import jax
import jax.numpy as jnp
from jax import lax

C = 256
FEAT_H = 64
FEAT_W = 64
PIXELS = 4096
FRAMES = 8
TRACKS = 512


def draw_frames(key, part):
    subkeys = jax.random.split(key, 1)
    values = jnp.clip(jax.random.normal(subkeys[0], (FRAMES, PIXELS, C), jnp.float32), -4.5, 4.5)
    return values.astype(jnp.bfloat16)


def plant(result, rng, low, high):
    spot = [jax.random.randint(jax.random.fold_in(rng, axis), (), 0, length) for axis, length in enumerate(result.shape)]
    main_axis = result.shape.index(max(result.shape))
    beside = spot[:main_axis] + [(spot[main_axis] + 1) % result.shape[main_axis]] + spot[main_axis + 1:]
    return result.at[tuple(spot)].set(low).at[tuple(beside)].set(high)


def block_scale(stream_key, shape, cuts, low, largest):
    def one(axis_at, parts):
        draws = jax.random.uniform(jax.random.fold_in(jax.random.fold_in(stream_key, 6), axis_at), (parts,), jnp.float32, low / len(cuts), largest / len(cuts))
        return jnp.repeat(jnp.exp(draws), shape[axis_at] // parts).reshape((-1,) + (1,) * (len(shape) - axis_at - 1))

    level = one(*cuts[0])
    for cut in cuts[1:]:
        level = level * one(*cut)
    return level


def bell_draw(own_key, shape, width, bound, shards=(), dtype=jnp.bfloat16):
    values = jax.random.normal(own_key, shape, jnp.float32) * width
    if len(shards) > 0:
        values = block_scale(own_key, shape, shards, -0.22, 0.18) * values
    return jnp.clip(values, min=-bound, max=bound).astype(dtype)


def setup_inputs(seed: int = 0, part: int = 0) -> dict:
    seeds = jax.random.split(jax.random.key(seed), 5)
    part_keys = jax.random.split(jax.random.fold_in(seeds[4], part), 5)
    return {
        "frames": draw_frames(jax.random.fold_in(jax.random.fold_in(seeds[4], part), 71), part),
        "query_frame": plant(jax.random.randint(part_keys[1], (TRACKS,), 0, FRAMES), jax.random.fold_in(part_keys[1], 1), 0, FRAMES - 1).astype(jnp.int32),
        "query_pixel": plant(jax.random.randint(part_keys[2], (TRACKS,), 0, PIXELS), jax.random.fold_in(part_keys[2], 1), 0, PIXELS - 1).astype(jnp.int32),
        "cotangent": bell_draw(part_keys[3], (2, FRAMES, TRACKS), 8.0, 48.0, ((1, 4), (2, 4)), jnp.float32),
    }


def reference(frames, query_frame, query_pixel, cotangent):
    all_pixels = frames.reshape(FRAMES * PIXELS, C)
    row_index = (query_frame * PIXELS + query_pixel).astype(jnp.int32)
    query_feat = all_pixels[row_index]
    score_scale = C ** -0.5
    pixel_ids = jnp.arange(PIXELS)
    coord_x = ((pixel_ids % FEAT_W) * (2.0 / (FEAT_W - 1)) - 1.0).astype(jnp.float32)
    coord_y = ((pixel_ids // FEAT_W) * (2.0 / (FEAT_H - 1)) - 1.0).astype(jnp.float32)

    def per_frame(total_grad, inputs):
        one_frame, frame_cot = inputs
        scores = jnp.dot(query_feat, one_frame.T, preferred_element_type=jnp.float32) * score_scale
        peak_score = jnp.max(scores, axis=1, keepdims=True)
        exp_scores = jnp.exp(scores - peak_score)
        weights = exp_scores / jnp.sum(exp_scores, axis=1, keepdims=True)
        expect_x = jnp.sum(weights * coord_x[None, :], axis=1)
        expect_y = jnp.sum(weights * coord_y[None, :], axis=1)
        grad_x = frame_cot[0]
        grad_y = frame_cot[1]
        inner_sum = grad_x * expect_x + grad_y * expect_y
        cost_grad = (weights * (grad_x[:, None] * coord_x[None, :] + grad_y[:, None] * coord_y[None, :] - inner_sum[:, None]) * score_scale).astype(jnp.bfloat16)
        image_grad = jnp.dot(cost_grad.T, query_feat, preferred_element_type=jnp.float32)
        total_grad = total_grad + jnp.dot(cost_grad, one_frame, preferred_element_type=jnp.float32)
        return total_grad, image_grad

    query_grad, frame_grads = lax.scan(per_frame, jnp.zeros((TRACKS, C), jnp.float32), (frames, jnp.moveaxis(cotangent, 1, 0)))
    frame_grad = jnp.transpose(frame_grads, (1, 0, 2))
    return frame_grad, query_grad
```

```python
import functools
import math

import jax
import jax.numpy as jnp
from jax import lax
from jax.experimental import pallas as pl
from jax.experimental.pallas import tpu as pltpu
from jax.sharding import PartitionSpec as P

C = 256
FEAT_H = 64
FEAT_W = 64
LANES = 128
LOG2E = math.log2(math.e)
F32 = jnp.float32
BF16 = jnp.bfloat16

COPY_ROWS = 1024
PICK_COLS = 1024
SCORE_COLS = 512
BLOCK_ROWS = 32
NT = (((1,), (1,)), ((), ()))
VMEM_SPEC = pl.BlockSpec(memory_space=pltpu.VMEM)
HBM_SPEC = pl.BlockSpec(memory_space=pltpu.HBM)
SMEM_SPEC = pl.BlockSpec(memory_space=pltpu.SMEM)
PARAMS = pltpu.CompilerParams(vmem_limit_bytes=40 << 20)


def xor_permute(value, axis, size, distance):
    return lax.ppermute(value, axis, [(i, i ^ distance) for i in range(size)])


def column_tile(row):
    return jnp.transpose(jnp.broadcast_to(row, (LANES, row.shape[1])))


def pick_kernel(held, pixels, place, frame_ref, pixel_ref, frames_hbm, frames_out, picked_ref, sems):
    rows = held * pixels
    count = rows // COPY_ROWS
    copies = [
        pltpu.make_async_copy(
            frames_hbm.at[pl.ds(i * COPY_ROWS, COPY_ROWS), :],
            frames_out.at[pl.ds(i * COPY_ROWS, COPY_ROWS), :],
            sems.at[i],
        )
        for i in range(count)
    ]
    for copy in copies:
        copy.start()
    local = frame_ref[...] - place[0] * held
    inside = (local >= 0) & (local < held)
    index = jnp.where(inside, local * pixels + pixel_ref[...], -1)
    tracks = index.shape[1]
    column = column_tile(index)
    lane = lax.broadcasted_iota(jnp.int32, (tracks, LANES), 1)
    total = jnp.zeros((tracks, picked_ref.shape[1]), F32)
    for i, copy in enumerate(copies):
        copy.wait()
        for start in range(i * COPY_ROWS, (i + 1) * COPY_ROWS, PICK_COLS):
            hits = [
                jnp.where(column - (start + at) == lane, 1.0, 0.0).astype(BF16)
                for at in range(0, PICK_COLS, LANES)
            ]
            total += jnp.dot(
                jnp.concatenate(hits, axis=1),
                frames_out[pl.ds(start, PICK_COLS), :],
                preferred_element_type=F32,
            )
    picked_ref[...] = total.astype(BF16)


def track_kernel(held, pixels, place, parts, feat_ref, frames_ref, cot_ref, stats_ref, *rest):
    part_refs, scores, term = rest[: parts], rest[parts], rest[parts + 1]
    tracks = feat_ref.shape[0]
    scale = C ** (-0.5)
    lane = lax.broadcasted_iota(jnp.int32, (1, LANES), 1)
    rows_per_tile = LANES // FEAT_W
    lane_x = (lane % FEAT_W).astype(F32) * (2.0 / (FEAT_W - 1)) - 1.0
    lane_y = (lane // FEAT_W).astype(F32) * (2.0 / (FEAT_H - 1)) - 1.0
    step_y = rows_per_tile * (2.0 / (FEAT_H - 1))
    feat = feat_ref[...]
    total = jnp.zeros(term.shape, F32)
    stat_rows = []
    for t in range(held):
        base = t * pixels
        peak = jnp.full((tracks, LANES), -jnp.inf, F32)
        for start in range(0, pixels, SCORE_COLS):
            block = lax.dot_general(
                feat, frames_ref[pl.ds(base + start, SCORE_COLS), :], NT, preferred_element_type=F32
            ) * (scale * LOG2E)
            scores[:, pl.ds(base + start, SCORE_COLS)] = block
            for at in range(0, SCORE_COLS, LANES):
                peak = jnp.maximum(peak, block[:, at : at + LANES])
        peak = jnp.broadcast_to(jnp.max(peak, axis=1, keepdims=True), (tracks, LANES))
        grad_x = column_tile(cot_ref[0, pl.ds(t, 1), :])
        grad_y = column_tile(cot_ref[1, pl.ds(t, 1), :])
        coefs = []
        for first in range(0, tracks, BLOCK_ROWS):
            lines = pl.ds(first, BLOCK_ROWS)
            top = peak[first : first + BLOCK_ROWS]
            sums = jnp.zeros((BLOCK_ROWS, LANES), F32)
            sums_y = jnp.zeros((BLOCK_ROWS, LANES), F32)
            for tile in range(pixels // LANES):
                cols = pl.ds(base + tile * LANES, LANES)
                power = jnp.exp2(scores[lines, cols] - top)
                scores[lines, cols] = power
                sums += power
                sums_y += power * (tile * step_y)
            norm = jnp.sum(sums, axis=1, keepdims=True)
            inverse = 1.0 / norm
            expect_x = jnp.sum(sums * lane_x, axis=1, keepdims=True) * inverse
            expect_y = jnp.sum(sums_y + sums * lane_y, axis=1, keepdims=True) * inverse
            gx = grad_x[first : first + BLOCK_ROWS]
            gy = grad_y[first : first + BLOCK_ROWS]
            factor = inverse * scale
            inner = (gx * expect_x + gy * expect_y) * factor
            gx = gx * factor
            gy = gy * factor
            coefs.append((gx, gy, inner))
        gx, gy, inner = (jnp.concatenate(list(c), axis=0) for c in zip(*coefs))
        table = gx * lane_x + gy * lane_y - inner
        for value in (peak, gx, gy, inner):
            stat_rows.append(jnp.transpose(value)[0:1])
        for start in range(0, pixels, SCORE_COLS):
            grads = []
            for at in range(start, start + SCORE_COLS, LANES):
                power = scores[:, pl.ds(base + at, LANES)]
                grads.append((power * (table + gy * ((at // LANES) * step_y))).astype(BF16))
            total += jnp.dot(
                jnp.concatenate(grads, axis=1),
                frames_ref[pl.ds(base + start, SCORE_COLS), :],
                preferred_element_type=F32,
            )
    stats_ref[...] = jnp.concatenate(stat_rows, axis=0)
    term[...] = total
    share = tracks // parts
    for i, part in enumerate(part_refs):
        owner = place[0] ^ i
        part[...] = term[pl.ds(pl.multiple_of(owner * share, share), share), :]


def frame_kernel(held, pixels, blocks, place, *refs):
    feat_refs, stat_refs = refs[:blocks], refs[blocks : 2 * blocks]
    frames_ref, out_ref = refs[2 * blocks], refs[2 * blocks + 1]
    scale = C ** (-0.5)
    own = out_ref.shape[0] // (held * (C // LANES))
    start_row = place[1] * own
    image_row0 = (start_row // FEAT_W).astype(F32)
    line_x = (lax.broadcasted_iota(jnp.int32, (FEAT_W, LANES), 0)).astype(F32) * (2.0 / (FEAT_W - 1)) - 1.0
    feats = [ref[...] for ref in feat_refs]
    tracks = feats[0].shape[0]
    everyone = jnp.concatenate(feats, axis=0)
    chunk = min(own, 256)
    for t in range(held):
        tables, peaks, slopes, inners = [], [], [], []
        for ref in stat_refs:
            for at in range(0, tracks, LANES):
                row = lambda k: ref[pl.ds(4 * t + k, 1), pl.ds(at, LANES)]
                peaks.append(row(0))
                tables.append(row(1) * line_x)
                slopes.append(row(2))
                inners.append(row(3))
        for first in range(0, own, chunk):
            lines = frames_ref[pl.ds(pl.multiple_of(t * pixels + start_row + first, FEAT_W), chunk), :]
            score = lax.dot_general(lines, everyone, NT, preferred_element_type=F32) * (scale * LOG2E)
            images = []
            for image in range(chunk // FEAT_W):
                coord_y = (image_row0 + (first // FEAT_W + image)) * (2.0 / (FEAT_H - 1)) - 1.0
                grads = []
                for b in range(len(peaks)):
                    part = score[image * FEAT_W : (image + 1) * FEAT_W, b * LANES : (b + 1) * LANES]
                    power = jnp.exp2(part - peaks[b])
                    grads.append((power * (tables[b] + (slopes[b] * coord_y - inners[b]))).astype(BF16))
                images.append(jnp.concatenate(grads, axis=1))
            grad = jnp.concatenate(images, axis=0)
            value = jnp.dot(grad, everyone, preferred_element_type=F32)
            lanes_tiles = C // LANES
            for k in range(lanes_tiles):
                out_ref[pl.ds(first * held * lanes_tiles + k * held + t, chunk, stride=held * lanes_tiles), :] = value[
                    :, k * LANES : (k + 1) * LANES
                ]


def on_device(sizes, frames, query_frame, query_pixel, cotangent):
    ranks, columns = sizes["frame"], sizes["track"]
    held, pixels, channels = frames.shape
    tracks = query_frame.shape[0]
    place = jnp.stack([lax.axis_index("frame"), lax.axis_index("track")]).astype(jnp.int32)
    flat = pltpu.with_memory_space_constraint(frames.reshape(held * pixels, channels), pltpu.HBM)

    kept, feat = pl.pallas_call(
        functools.partial(pick_kernel, held, pixels),
        out_shape=(pltpu.VMEM((held * pixels, channels), BF16), pltpu.VMEM((tracks, channels), BF16)),
        in_specs=[SMEM_SPEC, VMEM_SPEC, VMEM_SPEC, HBM_SPEC],
        out_specs=(VMEM_SPEC, VMEM_SPEC),
        scratch_shapes=[pltpu.SemaphoreType.DMA((held * pixels // COPY_ROWS,))],
        compiler_params=PARAMS,
        name="pick",
    )(place, query_frame[None], query_pixel[None], flat)

    distance = 1
    while distance < ranks:
        feat = feat + xor_permute(feat, "frame", ranks, distance)
        distance *= 2

    share = tracks // ranks
    stats, *terms = pl.pallas_call(
        lambda place_ref, *refs: track_kernel(held, pixels, place_ref, ranks, *refs),
        out_shape=(pltpu.VMEM((4 * held, tracks), F32),)
        + tuple(pltpu.VMEM((share, channels), F32) for _ in range(ranks)),
        in_specs=[SMEM_SPEC, VMEM_SPEC, VMEM_SPEC, VMEM_SPEC],
        out_specs=(VMEM_SPEC,) * (1 + ranks),
        scratch_shapes=[pltpu.VMEM((tracks, held * pixels), F32), pltpu.VMEM((tracks, channels), F32)],
        compiler_params=PARAMS,
        name="own_tracks",
    )(place, feat, kept, cotangent)

    feats, all_stats = [feat], [stats]
    for step in range(1, columns):
        feats.append(xor_permute(feat, "track", columns, step))
        all_stats.append(xor_permute(stats, "track", columns, step))
    query_grad = terms[0]
    arrived = [xor_permute(terms[i], "frame", ranks, i) for i in range(1, ranks)]

    own = pixels // columns
    frame_grad = pl.pallas_call(
        lambda place_ref, *refs: frame_kernel(held, pixels, columns, place_ref, *refs),
        out_shape=jax.ShapeDtypeStruct((own * held * channels // LANES, LANES), F32),
        in_specs=[SMEM_SPEC] + [VMEM_SPEC] * (2 * columns + 1),
        out_specs=VMEM_SPEC,
        compiler_params=PARAMS,
        cost_estimate=pl.CostEstimate(
            flops=4 * held * own * tracks * columns * channels,
            bytes_accessed=4 * held * own * channels,
            transcendentals=held * own * tracks * columns,
        ),
        name="own_pixels",
    )(place, *feats, *all_stats, kept)
    frame_grad = frame_grad.reshape(own, channels // LANES, held, LANES)
    frame_grad = jnp.transpose(frame_grad, (0, 2, 1, 3)).reshape(own, held, channels)
    for value in arrived:
        query_grad = query_grad + value
    return (frame_grad, query_grad)


def solution(mesh):
    return jax.shard_map(
        functools.partial(on_device, dict(mesh.shape)),
        mesh=mesh,
        in_specs=(
            P(("groups", "frame"), None, None),
            P(("groups", "track")),
            P(("groups", "track")),
            P(None, ("groups", "frame"), "track"),
        ),
        out_specs=(P("track", ("groups", "frame"), None), P(("groups", "track", "frame"), None)),
        check_vma=False,
    )
```

```python
import functools
import math

import jax
import jax.numpy as jnp
from jax import lax
from jax.experimental import pallas as pl
from jax.experimental.pallas import tpu as pltpu
from jax.sharding import PartitionSpec as P


C = 256
FEAT_H = 64
FEAT_W = 64
LANES = 128
ROW_TILE = 16
LOG2E = math.log2(math.e)
F32 = jnp.float32
BF16 = jnp.bfloat16

COPY_ROWS = 1024
PICK_COLS = 1024
PIXEL_ROWS = 256
BLOCK_ROWS = 8
STEPS = 4
FLIP_ROWS = 256
NT = (((1,), (1,)), ((), ()))
VMEM_SPEC = pl.BlockSpec(memory_space=pltpu.VMEM)
HBM_SPEC = pl.BlockSpec(memory_space=pltpu.HBM)
SMEM_SPEC = pl.BlockSpec(memory_space=pltpu.SMEM)
PARAMS = pltpu.CompilerParams(vmem_limit_bytes=40 << 20)


def xor_permute(value, axis, size, distance):
    return lax.ppermute(value, axis, [(i, i ^ distance) for i in range(size)])


def column_tile(row):
    return jnp.transpose(jnp.broadcast_to(row, (LANES, row.shape[1])))


def pack_stats(stats, channels):
    high = stats.astype(BF16)
    rest = stats - high.astype(F32)
    middle = rest.astype(BF16)
    low = (rest - middle.astype(F32)).astype(BF16)
    pieces = jnp.concatenate([high.astype(F32), middle.astype(F32), low.astype(F32)], axis=0)
    wide = []
    for at in range(0, stats.shape[1], LANES):
        wide.append(pieces[:, at : at + LANES])
    pieces = jnp.concatenate(wide, axis=0)
    rows = -(-pieces.shape[0] // ROW_TILE) * ROW_TILE
    if rows > pieces.shape[0]:
        pieces = jnp.concatenate([pieces, jnp.zeros((rows - pieces.shape[0], LANES), F32)], axis=0)
    return jnp.concatenate([pieces, jnp.zeros((rows, channels - LANES), F32)], axis=1).astype(BF16)


def unpack_stats(rows, count, tracks):
    rows = rows[:, :LANES].astype(F32)
    result = []
    for i in range(tracks // LANES):
        first = 3 * count * i
        high, middle, low = (rows[first + k * count : first + (k + 1) * count] for k in range(3))
        result.append((high + middle) + low)
    return result


def stat_rows_of(held, tracks):
    return -(-3 * 4 * held * (tracks // LANES) // ROW_TILE) * ROW_TILE


def pick_kernel(held, pixels, place, frame_hbm, pixel_hbm, frames_hbm, frames_out, picked_ref, queries, sems):
    rows = held * pixels
    count = rows // COPY_ROWS
    lookups = [
        pltpu.make_async_copy(ref, queries.at[pl.ds(i, 1), :], sems.at[count + i])
        for i, ref in enumerate((frame_hbm, pixel_hbm))
    ]
    for copy in lookups:
        copy.start()
    copies = [
        pltpu.make_async_copy(
            frames_hbm.at[pl.ds(i * COPY_ROWS, COPY_ROWS), :],
            frames_out.at[pl.ds(i * COPY_ROWS, COPY_ROWS), :],
            sems.at[i],
        )
        for i in range(count)
    ]
    for copy in copies:
        copy.start()
    for copy in lookups:
        copy.wait()
    local = queries[0:1, :] - place[0] * held
    inside = (local >= 0) & (local < held)
    index = jnp.where(inside, local * pixels + queries[1:2, :], -1)
    tracks = index.shape[1]
    column = column_tile(index)
    lane = lax.broadcasted_iota(jnp.int32, (tracks, LANES), 1)
    total = jnp.zeros((tracks, picked_ref.shape[1]), F32)
    for i, copy in enumerate(copies):
        copy.wait()
        for start in range(i * COPY_ROWS, (i + 1) * COPY_ROWS, PICK_COLS):
            hits = [
                jnp.where(column - (start + at) == lane, 1.0, 0.0).astype(BF16)
                for at in range(0, PICK_COLS, LANES)
            ]
            total += jnp.dot(
                jnp.concatenate(hits, axis=1),
                frames_out[pl.ds(start, PICK_COLS), :],
                preferred_element_type=F32,
            )
    picked_ref[...] = total.astype(BF16)


def flip_kernel(frames_ref, flipped_ref):
    for start in range(0, frames_ref.shape[0], FLIP_ROWS):
        flipped_ref[:, pl.ds(start, FLIP_ROWS)] = jnp.transpose(frames_ref[pl.ds(start, FLIP_ROWS), :])


def track_kernel(held, pixels, place, parts, feat_ref, frames_ref, flipped_ref, cot_ref, packed_ref, *rest):
    part_refs, rest = rest[: -6 - held], rest[-6 - held :]
    scores, (terms, peaks, sums, ordinals, tables, slopes) = rest[:held], rest[held:]
    tracks = feat_ref.shape[0]
    scale = C ** (-0.5)
    lane = lax.broadcasted_iota(jnp.int32, (1, LANES), 1)
    lane_x = (lane % FEAT_W).astype(F32) * (2.0 / (FEAT_W - 1)) - 1.0
    lane_y = (lane // FEAT_W).astype(F32) * (2.0 / (FEAT_H - 1)) - 1.0
    step_y = (LANES // FEAT_W) * (2.0 / (FEAT_H - 1))
    tiles = pixels // LANES
    width = pixels // STEPS
    height = tracks // STEPS
    feat = feat_ref[...]

    def score_unit(t, step):
        start = step * width
        if not isinstance(step, int):
            start = pl.multiple_of(start, width)
        block = jnp.dot(feat, flipped_ref[:, pl.ds(t * pixels + start, width)], preferred_element_type=F32)
        scores[t][:, pl.ds(start, width)] = block
        peak = peaks[t]
        for at in range(0, width, LANES):
            peak = jnp.maximum(peak, block[:, at : at + LANES])
        peaks[t] = peak

    def peak_unit(t):
        peaks[t] = jnp.broadcast_to(jnp.max(peaks[t], axis=1, keepdims=True) * (scale * LOG2E), (tracks, LANES))

    def soft_unit(t, step):
        for first in range(0, height, BLOCK_ROWS):
            lines = pl.ds(pl.multiple_of(step * height + first, BLOCK_ROWS), BLOCK_ROWS)
            top = peaks[t, lines, :]
            pending, odd = {}, {}
            for tile in range(tiles):
                cols = pl.ds(tile * LANES, LANES)
                value = jnp.exp2(scores[t][lines, cols] * (scale * LOG2E) - top)
                scores[t][lines, cols] = value
                level = 0
                while tile >> level & 1:
                    odd[level] = value if level not in odd else odd[level] + value
                    value = pending.pop(level) + value
                    level += 1
                pending[level] = value
            (total,) = pending.values()
            ordinal = odd[0]
            for level in range(1, len(odd)):
                ordinal = ordinal + odd[level] * float(1 << level)
            sums[lines, :] = total
            ordinals[lines, :] = ordinal

    def table_unit(t):
        total = sums[...]
        gx, gy = (column_tile(cot_ref[k, pl.ds(t, 1), :]) for k in range(2))
        inverse = 1.0 / jnp.sum(total, axis=1, keepdims=True)
        expect_x = jnp.sum(total * lane_x, axis=1, keepdims=True) * inverse
        expect_y = jnp.sum(ordinals[...] * step_y + total * lane_y, axis=1, keepdims=True) * inverse
        factor = inverse * scale
        slopes[...] = gy * (factor * step_y)
        gx, gy, inner = gx * factor, gy * factor, (gx * expect_x + gy * expect_y) * factor
        for value in (peaks[t], gx, gy, inner):
            stat_rows.append(jnp.transpose(value)[0:1])
        tables[...] = gx * lane_x + gy * lane_y - inner

    def grad_unit(t, step):
        table, slope = tables[...], slopes[...]
        half = width // 2
        for k in range(2):
            start = step * width + k * half
            coef = table + slope * (jnp.asarray(step * (width // LANES), F32) + float(k * half // LANES))
            grads = []
            if not isinstance(step, int):
                start = pl.multiple_of(start, half)
            for at in range(0, half, LANES):
                cols = start + at
                cols = cols if isinstance(step, int) else pl.multiple_of(cols, LANES)
                grads.append((scores[t][:, pl.ds(cols, LANES)] * coef).astype(BF16))
                coef = coef + slope
            terms[k] += jnp.dot(
                jnp.concatenate(grads, axis=1),
                frames_ref[pl.ds(t * pixels + start, half), :],
                preferred_element_type=F32,
            )

    stat_rows = []
    terms[...] = jnp.zeros(terms.shape, F32)
    peaks[...] = jnp.full(peaks.shape, -jnp.inf, F32)
    for step in range(STEPS):
        score_unit(0, step)
    for t in range(held):
        peak_unit(t)

        def body(step, carry, t=t):
            if t:
                grad_unit(t - 1, step)
            soft_unit(t, step)
            if t + 1 < held:
                score_unit(t + 1, step)
            return carry

        for step in range(STEPS):
            body(step, 0)
        table_unit(t)
    for step in range(STEPS):
        grad_unit(held - 1, step)
    packed_ref[pl.ds(0, tracks), :] = feat
    packed_ref[pl.ds(tracks, packed_ref.shape[0] - tracks), :] = pack_stats(jnp.concatenate(stat_rows, axis=0), feat.shape[1])
    terms[0] += terms[1]
    share = tracks // parts
    for i, part in enumerate(part_refs):
        owner = place[0] ^ i
        part[...] = terms[0, pl.ds(pl.multiple_of(owner * share, share), share), :]


def frame_kernel(held, pixels, own, tracks, place, block_refs, frames_ref, emit):
    scale = C ** (-0.5)
    start_row = place[1] * own
    image_row0 = (start_row // FEAT_W).astype(F32)
    line_x = (lax.broadcasted_iota(jnp.int32, (FEAT_W, LANES), 0)).astype(F32) * (2.0 / (FEAT_W - 1)) - 1.0
    everyone = jnp.concatenate([ref[pl.ds(0, tracks), :] for ref in block_refs], axis=0)
    stats = []
    for ref in block_refs:
        stats += unpack_stats(ref[pl.ds(tracks, ref.shape[0] - tracks), :], 4 * held, tracks)
    chunk = min(own, PIXEL_ROWS)
    units = [(first, t) for first in range(0, own, chunk) for t in range(held)]

    def score_of(first, t):
        lines = frames_ref[pl.ds(pl.multiple_of(t * pixels + start_row + first, FEAT_W), chunk), :]
        return lax.dot_general(lines, everyone, NT, preferred_element_type=F32) * (scale * LOG2E)

    def grad_of(first, t, score):
        images = []
        for image in range(chunk // FEAT_W):
            coord_y = (image_row0 + (first // FEAT_W + image)) * (2.0 / (FEAT_H - 1)) - 1.0
            grads = []
            for b, stat in enumerate(stats):
                peak, gx, gy, inner = (stat[4 * t + k : 4 * t + k + 1] for k in range(4))
                part = score[image * FEAT_W : (image + 1) * FEAT_W, b * LANES : (b + 1) * LANES]
                power = jnp.exp2(part - peak)
                grads.append((power * (gx * line_x + (gy * coord_y - inner))).astype(BF16))
            images.append(jnp.concatenate(grads, axis=1))
        return jnp.concatenate(images, axis=0)

    for unit in units:
        emit(*unit, jnp.dot(grad_of(*unit, score_of(*unit)), everyone, preferred_element_type=F32))


def pixel_kernel(held, pixels, tracks, place, *refs):
    block_refs, (frames_ref, out_hbm, out, sems) = refs[:-4], refs[-4:]
    lane_tiles = C // LANES
    lines_out = held * lane_tiles
    own = out.shape[0] // lines_out
    copies = []

    def emit(first, t, value):
        chunk = value.shape[0]
        for k in range(lane_tiles):
            out[pl.ds(first * lines_out + k * held + t, chunk, stride=lines_out), :] = value[
                :, k * LANES : (k + 1) * LANES
            ]
        if t == held - 1:
            rows = pl.ds(first * lines_out, chunk * lines_out)
            copy = pltpu.make_async_copy(out.at[rows, :], out_hbm.at[rows, :], sems.at[first // chunk])
            copy.start()
            copies.append(copy)

    frame_kernel(held, pixels, own, tracks, place, block_refs, frames_ref, emit)
    for copy in copies:
        copy.wait()


def on_device(sizes, frames, query_frame, query_pixel, cotangent):
    return steps_on_device(sizes, frames, query_frame, query_pixel, cotangent)


def steps_on_device(sizes, frames, query_frame, query_pixel, cotangent):
    ranks, columns = sizes["frame"], sizes["track"]
    held, pixels, channels = frames.shape
    tracks = query_frame.shape[0]
    place = jnp.stack([lax.axis_index("frame"), lax.axis_index("track")]).astype(jnp.int32)
    frames_hbm, frame_hbm, pixel_hbm = (
        pltpu.with_memory_space_constraint(value, pltpu.HBM)
        for value in (frames.reshape(held * pixels, channels), query_frame[None], query_pixel[None])
    )

    kept, feat = pl.pallas_call(
        functools.partial(pick_kernel, held, pixels),
        out_shape=(pltpu.VMEM((held * pixels, channels), BF16), pltpu.VMEM((tracks, channels), BF16)),
        in_specs=[SMEM_SPEC, HBM_SPEC, HBM_SPEC, HBM_SPEC],
        out_specs=(VMEM_SPEC, VMEM_SPEC),
        scratch_shapes=[
            pltpu.VMEM((2, tracks), jnp.int32),
            pltpu.SemaphoreType.DMA((held * pixels // COPY_ROWS + 2,)),
        ],
        compiler_params=PARAMS,
        name="pick",
    )(place, frame_hbm, pixel_hbm, frames_hbm)

    picks = [feat]
    for i in range(1, ranks):
        picks.append(xor_permute(feat, "frame", ranks, i))
    flipped = pl.pallas_call(
        flip_kernel,
        out_shape=pltpu.VMEM((channels, held * pixels), BF16),
        in_specs=[VMEM_SPEC],
        out_specs=VMEM_SPEC,
        compiler_params=PARAMS,
        cost_estimate=pl.CostEstimate(flops=0, bytes_accessed=4 * held * pixels * channels, transcendentals=0),
        name="flip",
    )(kept)
    feat = sum(picks[1:], picks[0])

    share = tracks // ranks
    packed, *terms = pl.pallas_call(
        lambda place_ref, *refs: track_kernel(held, pixels, place_ref, ranks, *refs),
        out_shape=(pltpu.VMEM((tracks + stat_rows_of(held, tracks), channels), BF16),)
        + tuple(pltpu.VMEM((share, channels), F32) for _ in range(ranks)),
        in_specs=[SMEM_SPEC, VMEM_SPEC, VMEM_SPEC, VMEM_SPEC, VMEM_SPEC],
        out_specs=(VMEM_SPEC,) * (1 + ranks),
        scratch_shapes=[
            *[pltpu.VMEM((tracks, pixels), F32)] * held,
            pltpu.VMEM((2, tracks, channels), F32),
            pltpu.VMEM((held, tracks, LANES), F32),
        ]
        + [pltpu.VMEM((tracks, LANES), F32)] * 4,
        compiler_params=PARAMS,
        name="own_tracks",
    )(place, feat, kept, flipped, cotangent)

    far_blocks, distance = [], columns // 2
    while distance > 1:
        far_blocks += [xor_permute(block, "track", columns, distance) for block in [packed] + far_blocks]
        distance //= 2
    arrived = []
    for i in range(1, ranks):
        arrived.append(xor_permute(terms[i], "frame", ranks, i))
    near_blocks = [packed, xor_permute(packed, "track", columns, 1)]

    own = pixels // columns
    lines_out = held * channels // LANES

    def cost(count):
        return pl.CostEstimate(
            flops=4 * held * own * tracks * count * channels,
            bytes_accessed=4 * held * own * channels,
            transcendentals=held * own * tracks * count,
        )

    far_blocks += [xor_permute(block, "track", columns, 1) for block in far_blocks]
    query_grad = terms[0]

    frame_grad = pl.pallas_call(
        functools.partial(pixel_kernel, held, pixels, tracks),
        out_shape=jax.ShapeDtypeStruct((own * lines_out, LANES), F32),
        in_specs=[SMEM_SPEC] + [VMEM_SPEC] * (columns + 1),
        out_specs=HBM_SPEC,
        scratch_shapes=[
            pltpu.VMEM((own * lines_out, LANES), F32),
            pltpu.SemaphoreType.DMA((own // min(own, PIXEL_ROWS),)),
        ],
        compiler_params=PARAMS,
        cost_estimate=cost(columns),
        name="own_pixels",
    )(place, *near_blocks, *far_blocks, kept)
    frame_grad, query_grad, *arrived = lax.optimization_barrier((frame_grad, query_grad, *arrived))
    frame_grad = frame_grad.reshape(own, channels // LANES, held, LANES)
    frame_grad = jnp.transpose(frame_grad, (0, 2, 1, 3)).reshape(own, held, channels)
    for value in arrived:
        query_grad = query_grad + value
    return (frame_grad, query_grad)


def solution(mesh):
    return jax.shard_map(
        functools.partial(on_device, dict(mesh.shape)),
        mesh=mesh,
        in_specs=(
            P(("groups", "frame"), None, None),
            P(("groups", "track")),
            P(("groups", "track")),
            P(None, ("groups", "frame"), "track"),
        ),
        out_specs=(P("track", ("groups", "frame"), None), P(("groups", "track", "frame"), None)),
        check_vma=False,
    )
```

```python
import functools
import math

import jax
import jax.numpy as jnp
from jax import lax
from jax.experimental import pallas as pl
from jax.experimental.pallas import tpu as pltpu
from jax.sharding import PartitionSpec as P


C = 256
FEAT_H = 64
FEAT_W = 64
LANES = 128
ROW_TILE = 16
LOG2E = math.log2(math.e)
F32 = jnp.float32
BF16 = jnp.bfloat16

COPY_ROWS = 1024
PICK_COLS = 512
PIXEL_ROWS = 256
BLOCK_ROWS = 8
STEPS = 8
FLIP_ROWS = 256
NT = (((1,), (1,)), ((), ()))
VMEM_SPEC = pl.BlockSpec(memory_space=pltpu.VMEM)
HBM_SPEC = pl.BlockSpec(memory_space=pltpu.HBM)
SMEM_SPEC = pl.BlockSpec(memory_space=pltpu.SMEM)
PARAMS = pltpu.CompilerParams(vmem_limit_bytes=40 << 20)


def xor_permute(value, axis, size, distance):
    return lax.ppermute(value, axis, [(i, i ^ distance) for i in range(size)])


def column_tile(row):
    return jnp.transpose(jnp.broadcast_to(row, (LANES, row.shape[1])))


def pack_stats(stats, channels):
    high = stats.astype(BF16)
    rest = stats - high.astype(F32)
    middle = rest.astype(BF16)
    low = (rest - middle.astype(F32)).astype(BF16)
    pieces = jnp.concatenate([high.astype(F32), middle.astype(F32), low.astype(F32)], axis=0)
    wide = []
    for at in range(0, stats.shape[1], LANES):
        wide.append(pieces[:, at : at + LANES])
    pieces = jnp.concatenate(wide, axis=0)
    rows = -(-pieces.shape[0] // ROW_TILE) * ROW_TILE
    if rows > pieces.shape[0]:
        pieces = jnp.concatenate([pieces, jnp.zeros((rows - pieces.shape[0], LANES), F32)], axis=0)
    return jnp.concatenate([pieces, jnp.zeros((rows, channels - LANES), F32)], axis=1).astype(BF16)


def unpack_stats(rows, count, tracks):
    rows = rows[:, :LANES].astype(F32)
    result = []
    for i in range(tracks // LANES):
        first = 3 * count * i
        high, middle, low = (rows[first + k * count : first + (k + 1) * count] for k in range(3))
        result.append((high + middle) + low)
    return result


def stat_rows_of(held, tracks):
    return -(-3 * 4 * held * (tracks // LANES) // ROW_TILE) * ROW_TILE


def pick_kernel(held, pixels, place, frame_hbm, pixel_hbm, frames_hbm, frames_out, picked_ref, queries, totals, sems):
    rows = held * pixels
    count = rows // COPY_ROWS
    lookups = [
        pltpu.make_async_copy(ref, queries.at[pl.ds(i, 1), :], sems.at[count + i])
        for i, ref in enumerate((frame_hbm, pixel_hbm))
    ]
    for copy in lookups:
        copy.start()
    copies = [
        pltpu.make_async_copy(
            frames_hbm.at[pl.ds(i * COPY_ROWS, COPY_ROWS), :],
            frames_out.at[pl.ds(i * COPY_ROWS, COPY_ROWS), :],
            sems.at[i],
        )
        for i in range(count)
    ]
    for copy in copies:
        copy.start()
    for copy in lookups:
        copy.wait()
    local = queries[0:1, :] - place[0] * held
    inside = (local >= 0) & (local < held)
    index = jnp.where(inside, local * pixels + queries[1:2, :], -1)
    tracks = index.shape[1]
    column = column_tile(index)
    lane = lax.broadcasted_iota(jnp.int32, (tracks, LANES), 1)
    totals[...] = jnp.zeros(totals.shape, F32)
    for i, copy in enumerate(copies):
        copy.wait()
        for k, start in enumerate(range(i * COPY_ROWS, (i + 1) * COPY_ROWS, PICK_COLS)):
            hits = [
                jnp.where(column - (start + at) == lane, 1.0, 0.0).astype(BF16)
                for at in range(0, PICK_COLS, LANES)
            ]
            totals[k % 2] += jnp.dot(
                jnp.concatenate(hits, axis=1),
                frames_out[pl.ds(start, PICK_COLS), :],
                preferred_element_type=F32,
            )
    picked_ref[...] = (totals[0] + totals[1]).astype(BF16)


def flip_kernel(frames_ref, flipped_ref):
    for start in range(0, frames_ref.shape[0], FLIP_ROWS):
        flipped_ref[:, pl.ds(start, FLIP_ROWS)] = jnp.transpose(frames_ref[pl.ds(start, FLIP_ROWS), :])


def track_kernel(held, pixels, place, parts, feat_ref, frames_ref, flipped_ref, cot_ref, packed_ref, *rest):
    part_refs, rest = rest[: -6 - held], rest[-6 - held :]
    scores, (terms, peaks, sums, ordinals, tables, slopes) = rest[:held], rest[held:]
    tracks = feat_ref.shape[0]
    scale = C ** (-0.5)
    lane = lax.broadcasted_iota(jnp.int32, (1, LANES), 1)
    lane_x = (lane % FEAT_W).astype(F32) * (2.0 / (FEAT_W - 1)) - 1.0
    lane_y = (lane // FEAT_W).astype(F32) * (2.0 / (FEAT_H - 1)) - 1.0
    step_y = (LANES // FEAT_W) * (2.0 / (FEAT_H - 1))
    tiles = pixels // LANES
    width = pixels // STEPS
    height = tracks // STEPS
    feat = feat_ref[...]

    def score_unit(t, step):
        start = step * width
        if not isinstance(step, int):
            start = pl.multiple_of(start, width)
        block = jnp.dot(feat, flipped_ref[:, pl.ds(t * pixels + start, width)], preferred_element_type=F32)
        scores[t][:, pl.ds(start, width)] = block
        peak = peaks[t]
        for at in range(0, width, LANES):
            peak = jnp.maximum(peak, block[:, at : at + LANES])
        peaks[t] = peak

    def peak_unit(t):
        peaks[t] = jnp.broadcast_to(jnp.max(peaks[t], axis=1, keepdims=True) * (scale * LOG2E), (tracks, LANES))

    def soft_unit(t, step):
        for first in range(0, height, BLOCK_ROWS):
            lines = pl.ds(pl.multiple_of(step * height + first, BLOCK_ROWS), BLOCK_ROWS)
            top = peaks[t, lines, :]
            pending, odd = {}, {}
            for tile in range(tiles):
                cols = pl.ds(tile * LANES, LANES)
                value = jnp.exp2(scores[t][lines, cols] * (scale * LOG2E) - top)
                scores[t][lines, cols] = value
                level = 0
                while tile >> level & 1:
                    odd[level] = value if level not in odd else odd[level] + value
                    value = pending.pop(level) + value
                    level += 1
                pending[level] = value
            (total,) = pending.values()
            ordinal = odd[0]
            for level in range(1, len(odd)):
                ordinal = ordinal + odd[level] * float(1 << level)
            sums[lines, :] = total
            ordinals[lines, :] = ordinal

    def table_unit(t):
        total = sums[...]
        gx, gy = (column_tile(cot_ref[k, pl.ds(t, 1), :]) for k in range(2))
        inverse = 1.0 / jnp.sum(total, axis=1, keepdims=True)
        expect_x = jnp.sum(total * lane_x, axis=1, keepdims=True) * inverse
        expect_y = jnp.sum(ordinals[...] * step_y + total * lane_y, axis=1, keepdims=True) * inverse
        factor = inverse * scale
        slopes[...] = gy * (factor * step_y)
        gx, gy, inner = gx * factor, gy * factor, (gx * expect_x + gy * expect_y) * factor
        for value in (peaks[t], gx, gy, inner):
            stat_rows.append(jnp.transpose(value)[0:1])
        tables[...] = gx * lane_x + gy * lane_y - inner

    def grad_unit(t, step):
        table, slope = tables[...], slopes[...]
        half = width // 2
        for k in range(2):
            start = step * width + k * half
            coef = table + slope * (jnp.asarray(step * (width // LANES), F32) + float(k * half // LANES))
            grads = []
            if not isinstance(step, int):
                start = pl.multiple_of(start, half)
            for at in range(0, half, LANES):
                cols = start + at
                cols = cols if isinstance(step, int) else pl.multiple_of(cols, LANES)
                grads.append((scores[t][:, pl.ds(cols, LANES)] * coef).astype(BF16))
                coef = coef + slope
            terms[k] += jnp.dot(
                jnp.concatenate(grads, axis=1),
                frames_ref[pl.ds(t * pixels + start, half), :],
                preferred_element_type=F32,
            )

    stat_rows = []
    terms[...] = jnp.zeros(terms.shape, F32)
    peaks[...] = jnp.full(peaks.shape, -jnp.inf, F32)
    for step in range(STEPS):
        score_unit(0, step)
    for t in range(held):
        peak_unit(t)

        def body(step, carry, t=t):
            if t:
                grad_unit(t - 1, step)
            soft_unit(t, step)
            if t + 1 < held:
                score_unit(t + 1, step)
            return carry

        for step in range(STEPS):
            body(step, 0)
        table_unit(t)
    for step in range(STEPS):
        grad_unit(held - 1, step)
    packed_ref[pl.ds(0, tracks), :] = feat
    packed_ref[pl.ds(tracks, packed_ref.shape[0] - tracks), :] = pack_stats(jnp.concatenate(stat_rows, axis=0), feat.shape[1])
    terms[0] += terms[1]
    share = tracks // parts
    for i, part in enumerate(part_refs):
        owner = place[0] ^ i
        part[...] = terms[0, pl.ds(pl.multiple_of(owner * share, share), share), :]


def frame_kernel(held, pixels, own, tracks, place, block_refs, frames_ref, emit):
    scale = C ** (-0.5)
    start_row = place[1] * own
    image_row0 = (start_row // FEAT_W).astype(F32)
    line_x = (lax.broadcasted_iota(jnp.int32, (FEAT_W, LANES), 0)).astype(F32) * (2.0 / (FEAT_W - 1)) - 1.0
    everyone = jnp.concatenate([ref[pl.ds(0, tracks), :] for ref in block_refs], axis=0)
    stats = []
    for ref in block_refs:
        stats += unpack_stats(ref[pl.ds(tracks, ref.shape[0] - tracks), :], 4 * held, tracks)
    chunk = min(own, PIXEL_ROWS)
    units = [(first, t) for first in range(0, own, chunk) for t in range(held)]

    def score_of(first, t):
        lines = frames_ref[pl.ds(pl.multiple_of(t * pixels + start_row + first, FEAT_W), chunk), :]
        return lax.dot_general(lines, everyone, NT, preferred_element_type=F32) * (scale * LOG2E)

    def grad_of(first, t, score):
        images = []
        for image in range(chunk // FEAT_W):
            coord_y = (image_row0 + (first // FEAT_W + image)) * (2.0 / (FEAT_H - 1)) - 1.0
            grads = []
            for b, stat in enumerate(stats):
                peak, gx, gy, inner = (stat[4 * t + k : 4 * t + k + 1] for k in range(4))
                part = score[image * FEAT_W : (image + 1) * FEAT_W, b * LANES : (b + 1) * LANES]
                power = jnp.exp2(part - peak)
                grads.append((power * (gx * line_x + (gy * coord_y - inner))).astype(BF16))
            images.append(jnp.concatenate(grads, axis=1))
        return jnp.concatenate(images, axis=0)

    for unit in units:
        emit(*unit, jnp.dot(grad_of(*unit, score_of(*unit)), everyone, preferred_element_type=F32))


def pixel_kernel(held, pixels, tracks, place, *refs):
    block_refs, (frames_ref, out_hbm, out, sems) = refs[:-4], refs[-4:]
    lane_tiles = C // LANES
    lines_out = held * lane_tiles
    own = out.shape[0] // lines_out
    copies = []

    def emit(first, t, value):
        chunk = value.shape[0]
        for k in range(lane_tiles):
            out[pl.ds(first * lines_out + k * held + t, chunk, stride=lines_out), :] = value[
                :, k * LANES : (k + 1) * LANES
            ]
        if t == held - 1:
            rows = pl.ds(first * lines_out, chunk * lines_out)
            copy = pltpu.make_async_copy(out.at[rows, :], out_hbm.at[rows, :], sems.at[first // chunk])
            copy.start()
            copies.append(copy)

    frame_kernel(held, pixels, own, tracks, place, block_refs, frames_ref, emit)
    for copy in copies:
        copy.wait()


def on_device(sizes, frames, query_frame, query_pixel, cotangent):
    return steps_on_device(sizes, frames, query_frame, query_pixel, cotangent)


def steps_on_device(sizes, frames, query_frame, query_pixel, cotangent):
    ranks, columns = sizes["frame"], sizes["track"]
    held, pixels, channels = frames.shape
    tracks = query_frame.shape[0]
    place = jnp.stack([lax.axis_index("frame"), lax.axis_index("track")]).astype(jnp.int32)
    frames_hbm, frame_hbm, pixel_hbm = (
        pltpu.with_memory_space_constraint(value, pltpu.HBM)
        for value in (frames.reshape(held * pixels, channels), query_frame[None], query_pixel[None])
    )

    kept, feat = pl.pallas_call(
        functools.partial(pick_kernel, held, pixels),
        out_shape=(pltpu.VMEM((held * pixels, channels), BF16), pltpu.VMEM((tracks, channels), BF16)),
        in_specs=[SMEM_SPEC, HBM_SPEC, HBM_SPEC, HBM_SPEC],
        out_specs=(VMEM_SPEC, VMEM_SPEC),
        scratch_shapes=[
            pltpu.VMEM((2, tracks), jnp.int32),
            pltpu.VMEM((2, tracks, channels), F32),
            pltpu.SemaphoreType.DMA((held * pixels // COPY_ROWS + 2,)),
        ],
        compiler_params=PARAMS,
        name="pick",
    )(place, frame_hbm, pixel_hbm, frames_hbm)

    picks = [feat]
    for i in range(1, ranks):
        picks.append(xor_permute(feat, "frame", ranks, i))
    flipped = pl.pallas_call(
        flip_kernel,
        out_shape=pltpu.VMEM((channels, held * pixels), BF16),
        in_specs=[VMEM_SPEC],
        out_specs=VMEM_SPEC,
        compiler_params=PARAMS,
        cost_estimate=pl.CostEstimate(flops=0, bytes_accessed=4 * held * pixels * channels, transcendentals=0),
        name="flip",
    )(kept)
    feat = sum(picks[1:], picks[0])

    share = tracks // ranks
    packed, *terms = pl.pallas_call(
        lambda place_ref, *refs: track_kernel(held, pixels, place_ref, ranks, *refs),
        out_shape=(pltpu.VMEM((tracks + stat_rows_of(held, tracks), channels), BF16),)
        + tuple(pltpu.VMEM((share, channels), F32) for _ in range(ranks)),
        in_specs=[SMEM_SPEC, VMEM_SPEC, VMEM_SPEC, VMEM_SPEC, VMEM_SPEC],
        out_specs=(VMEM_SPEC,) * (1 + ranks),
        scratch_shapes=[
            *[pltpu.VMEM((tracks, pixels), F32)] * held,
            pltpu.VMEM((2, tracks, channels), F32),
            pltpu.VMEM((held, tracks, LANES), F32),
        ]
        + [pltpu.VMEM((tracks, LANES), F32)] * 4,
        compiler_params=PARAMS,
        name="own_tracks",
    )(place, feat, kept, flipped, cotangent)

    far_blocks, distance = [], columns // 2
    while distance > 1:
        far_blocks += [xor_permute(block, "track", columns, distance) for block in [packed] + far_blocks]
        distance //= 2
    arrived = []
    for i in range(1, ranks):
        arrived.append(xor_permute(terms[i], "frame", ranks, i))
    near_blocks = [packed, xor_permute(packed, "track", columns, 1)]

    own = pixels // columns
    lines_out = held * channels // LANES

    def cost(count):
        return pl.CostEstimate(
            flops=4 * held * own * tracks * count * channels,
            bytes_accessed=4 * held * own * channels,
            transcendentals=held * own * tracks * count,
        )

    far_blocks += [xor_permute(block, "track", columns, 1) for block in far_blocks]
    query_grad = terms[0]

    frame_grad = pl.pallas_call(
        functools.partial(pixel_kernel, held, pixels, tracks),
        out_shape=jax.ShapeDtypeStruct((own * lines_out, LANES), F32),
        in_specs=[SMEM_SPEC] + [VMEM_SPEC] * (columns + 1),
        out_specs=HBM_SPEC,
        scratch_shapes=[
            pltpu.VMEM((own * lines_out, LANES), F32),
            pltpu.SemaphoreType.DMA((own // min(own, PIXEL_ROWS),)),
        ],
        compiler_params=PARAMS,
        cost_estimate=cost(columns),
        name="own_pixels",
    )(place, *near_blocks, *far_blocks, kept)
    frame_grad, query_grad, *arrived = lax.optimization_barrier((frame_grad, query_grad, *arrived))
    frame_grad = frame_grad.reshape(own, channels // LANES, held, LANES)
    frame_grad = jnp.transpose(frame_grad, (0, 2, 1, 3)).reshape(own, held, channels)
    for value in arrived:
        query_grad = query_grad + value
    return (frame_grad, query_grad)


def solution(mesh):
    return jax.shard_map(
        functools.partial(on_device, dict(mesh.shape)),
        mesh=mesh,
        in_specs=(
            P(("groups", "frame"), None, None),
            P(("groups", "track")),
            P(("groups", "track")),
            P(None, ("groups", "frame"), "track"),
        ),
        out_specs=(P("track", ("groups", "frame"), None), P(("groups", "track", "frame"), None)),
        check_vma=False,
    )
```

```python
import functools
import math

import jax
import jax.numpy as jnp
from jax import lax
from jax.experimental import pallas as pl
from jax.experimental.pallas import tpu as pltpu
from jax.sharding import PartitionSpec as P


C = 256
FEAT_H = 64
FEAT_W = 64
LANES = 128
ROW_TILE = 16
LOG2E = math.log2(math.e)
F32 = jnp.float32
BF16 = jnp.bfloat16

COPY_ROWS = 1024
PICK_COLS = 512
PIXEL_ROWS = 256
BLOCK_ROWS = 8
STEPS = 8
FLIP_ROWS = 256
NT = (((1,), (1,)), ((), ()))
VMEM_SPEC = pl.BlockSpec(memory_space=pltpu.VMEM)
HBM_SPEC = pl.BlockSpec(memory_space=pltpu.HBM)
SMEM_SPEC = pl.BlockSpec(memory_space=pltpu.SMEM)
PARAMS = pltpu.CompilerParams(vmem_limit_bytes=40 << 20)


def xor_permute(value, axis, size, distance):
    return lax.ppermute(value, axis, [(i, i ^ distance) for i in range(size)])


def column_tile(row):
    return jnp.transpose(jnp.broadcast_to(row, (LANES, row.shape[1])))


def pack_stats(stats, channels):
    high = stats.astype(BF16)
    rest = stats - high.astype(F32)
    middle = rest.astype(BF16)
    low = (rest - middle.astype(F32)).astype(BF16)
    pieces = jnp.concatenate([high.astype(F32), middle.astype(F32), low.astype(F32)], axis=0)
    wide = []
    for at in range(0, stats.shape[1], LANES):
        wide.append(pieces[:, at : at + LANES])
    pieces = jnp.concatenate(wide, axis=0)
    fold = channels // LANES
    rows = -(-pieces.shape[0] // (fold * ROW_TILE)) * fold * ROW_TILE
    if rows > pieces.shape[0]:
        pieces = jnp.concatenate([pieces, jnp.zeros((rows - pieces.shape[0], LANES), F32)], axis=0)
    deep = rows // fold
    return jnp.concatenate([pieces[k * deep : (k + 1) * deep] for k in range(fold)], axis=1).astype(BF16)


def unpack_stats(rows, count, tracks):
    rows = jnp.concatenate([rows[:, at : at + LANES].astype(F32) for at in range(0, rows.shape[1], LANES)], axis=0)
    result = []
    for i in range(tracks // LANES):
        first = 3 * count * i
        high, middle, low = (rows[first + k * count : first + (k + 1) * count] for k in range(3))
        result.append((high + middle) + low)
    return result


def stat_rows_of(held, tracks):
    return -(-3 * 4 * held * (tracks // LANES) // (C // LANES * ROW_TILE)) * ROW_TILE


def pick_kernel(held, pixels, place, frame_hbm, pixel_hbm, frames_hbm, frames_out, picked_ref, queries, totals, sems):
    rows = held * pixels
    count = rows // COPY_ROWS
    lookups = [
        pltpu.make_async_copy(ref, queries.at[pl.ds(i, 1), :], sems.at[count + i])
        for i, ref in enumerate((frame_hbm, pixel_hbm))
    ]
    for copy in lookups:
        copy.start()
    copies = [
        pltpu.make_async_copy(
            frames_hbm.at[pl.ds(i * COPY_ROWS, COPY_ROWS), :],
            frames_out.at[pl.ds(i * COPY_ROWS, COPY_ROWS), :],
            sems.at[i],
        )
        for i in range(count)
    ]
    for copy in copies:
        copy.start()
    for copy in lookups:
        copy.wait()
    local = queries[0:1, :] - place[0] * held
    inside = (local >= 0) & (local < held)
    index = jnp.where(inside, local * pixels + queries[1:2, :], -1)
    tracks = index.shape[1]
    column = column_tile(index)
    lane = lax.broadcasted_iota(jnp.int32, (tracks, LANES), 1)
    totals[...] = jnp.zeros(totals.shape, F32)
    for i, copy in enumerate(copies):
        copy.wait()
        for k, start in enumerate(range(i * COPY_ROWS, (i + 1) * COPY_ROWS, PICK_COLS)):
            hits = [
                jnp.where(column - (start + at) == lane, 1.0, 0.0).astype(BF16)
                for at in range(0, PICK_COLS, LANES)
            ]
            totals[k % 2] += jnp.dot(
                jnp.concatenate(hits, axis=1),
                frames_out[pl.ds(start, PICK_COLS), :],
                preferred_element_type=F32,
            )
    picked_ref[...] = (totals[0] + totals[1]).astype(BF16)


def flip_kernel(frames_ref, flipped_ref):
    for start in range(0, frames_ref.shape[0], FLIP_ROWS):
        flipped_ref[:, pl.ds(start, FLIP_ROWS)] = jnp.transpose(frames_ref[pl.ds(start, FLIP_ROWS), :])


def track_kernel(held, pixels, place, parts, feat_ref, frames_ref, flipped_ref, cot_ref, packed_ref, *rest):
    part_refs, rest = rest[: -6 - held], rest[-6 - held :]
    scores, (terms, peaks, sums, ordinals, tables, slopes) = rest[:held], rest[held:]
    tracks = feat_ref.shape[0]
    scale = C ** (-0.5)
    lane = lax.broadcasted_iota(jnp.int32, (1, LANES), 1)
    lane_x = (lane % FEAT_W).astype(F32) * (2.0 / (FEAT_W - 1)) - 1.0
    lane_y = (lane // FEAT_W).astype(F32) * (2.0 / (FEAT_H - 1)) - 1.0
    step_y = (LANES // FEAT_W) * (2.0 / (FEAT_H - 1))
    tiles = pixels // LANES
    width = pixels // STEPS
    height = tracks // STEPS
    feat = feat_ref[...]

    def score_unit(t, step):
        start = step * width
        if not isinstance(step, int):
            start = pl.multiple_of(start, width)
        block = jnp.dot(feat, flipped_ref[:, pl.ds(t * pixels + start, width)], preferred_element_type=F32)
        scores[t][:, pl.ds(start, width)] = block
        peak = peaks[t]
        for at in range(0, width, LANES):
            peak = jnp.maximum(peak, block[:, at : at + LANES])
        peaks[t] = peak

    def peak_unit(t):
        peaks[t] = jnp.broadcast_to(jnp.max(peaks[t], axis=1, keepdims=True) * (scale * LOG2E), (tracks, LANES))

    def soft_unit(t, step):
        for first in range(0, height, BLOCK_ROWS):
            lines = pl.ds(pl.multiple_of(step * height + first, BLOCK_ROWS), BLOCK_ROWS)
            top = peaks[t, lines, :]
            pending, odd = {}, {}
            for tile in range(tiles):
                cols = pl.ds(tile * LANES, LANES)
                value = jnp.exp2(scores[t][lines, cols] * (scale * LOG2E) - top)
                scores[t][lines, cols] = value
                level = 0
                while tile >> level & 1:
                    odd[level] = value if level not in odd else odd[level] + value
                    value = pending.pop(level) + value
                    level += 1
                pending[level] = value
            (total,) = pending.values()
            ordinal = odd[0]
            for level in range(1, len(odd)):
                ordinal = ordinal + odd[level] * float(1 << level)
            sums[lines, :] = total
            ordinals[lines, :] = ordinal

    def table_unit(t):
        total = sums[...]
        gx, gy = (column_tile(cot_ref[k, pl.ds(t, 1), :]) for k in range(2))
        inverse = 1.0 / jnp.sum(total, axis=1, keepdims=True)
        expect_x = jnp.sum(total * lane_x, axis=1, keepdims=True) * inverse
        expect_y = jnp.sum(ordinals[...] * step_y + total * lane_y, axis=1, keepdims=True) * inverse
        factor = inverse * scale
        slopes[...] = gy * (factor * step_y)
        gx, gy, inner = gx * factor, gy * factor, (gx * expect_x + gy * expect_y) * factor
        for value in (peaks[t], gx, gy, inner):
            stat_rows.append(jnp.transpose(value)[0:1])
        tables[...] = gx * lane_x + gy * lane_y - inner

    def grad_unit(t, step):
        table, slope = tables[...], slopes[...]
        half = width // 2
        for k in range(2):
            start = step * width + k * half
            coef = table + slope * (jnp.asarray(step * (width // LANES), F32) + float(k * half // LANES))
            grads = []
            if not isinstance(step, int):
                start = pl.multiple_of(start, half)
            for at in range(0, half, LANES):
                cols = start + at
                cols = cols if isinstance(step, int) else pl.multiple_of(cols, LANES)
                grads.append((scores[t][:, pl.ds(cols, LANES)] * coef).astype(BF16))
                coef = coef + slope
            terms[k] += jnp.dot(
                jnp.concatenate(grads, axis=1),
                frames_ref[pl.ds(t * pixels + start, half), :],
                preferred_element_type=F32,
            )

    stat_rows = []
    terms[...] = jnp.zeros(terms.shape, F32)
    peaks[...] = jnp.full(peaks.shape, -jnp.inf, F32)
    for step in range(STEPS):
        score_unit(0, step)
    for t in range(held):
        peak_unit(t)

        def body(step, carry, t=t):
            if t:
                grad_unit(t - 1, step)
            soft_unit(t, step)
            if t + 1 < held:
                score_unit(t + 1, step)
            return carry

        for step in range(STEPS):
            body(step, 0)
        table_unit(t)
    for step in range(STEPS):
        grad_unit(held - 1, step)
    packed_ref[pl.ds(0, tracks), :] = feat
    packed_ref[pl.ds(tracks, packed_ref.shape[0] - tracks), :] = pack_stats(jnp.concatenate(stat_rows, axis=0), feat.shape[1])
    terms[0] += terms[1]
    share = tracks // parts
    for i, part in enumerate(part_refs):
        owner = place[0] ^ i
        part[...] = terms[0, pl.ds(pl.multiple_of(owner * share, share), share), :]


def frame_kernel(held, pixels, own, tracks, place, block_refs, frames_ref, emit):
    scale = C ** (-0.5)
    start_row = place[1] * own
    image_row0 = (start_row // FEAT_W).astype(F32)
    line_x = (lax.broadcasted_iota(jnp.int32, (FEAT_W, LANES), 0)).astype(F32) * (2.0 / (FEAT_W - 1)) - 1.0
    everyone = jnp.concatenate([ref[pl.ds(0, tracks), :] for ref in block_refs], axis=0)
    stats = []
    for ref in block_refs:
        stats += unpack_stats(ref[pl.ds(tracks, ref.shape[0] - tracks), :], 4 * held, tracks)
    chunk = min(own, PIXEL_ROWS)
    units = [(first, t) for first in range(0, own, chunk) for t in range(held)]

    def score_of(first, t):
        lines = frames_ref[pl.ds(pl.multiple_of(t * pixels + start_row + first, FEAT_W), chunk), :]
        return lax.dot_general(lines, everyone, NT, preferred_element_type=F32) * (scale * LOG2E)

    def grad_of(first, t, score):
        images = []
        for image in range(chunk // FEAT_W):
            coord_y = (image_row0 + (first // FEAT_W + image)) * (2.0 / (FEAT_H - 1)) - 1.0
            grads = []
            for b, stat in enumerate(stats):
                peak, gx, gy, inner = (stat[4 * t + k : 4 * t + k + 1] for k in range(4))
                part = score[image * FEAT_W : (image + 1) * FEAT_W, b * LANES : (b + 1) * LANES]
                power = jnp.exp2(part - peak)
                grads.append((power * (gx * line_x + (gy * coord_y - inner))).astype(BF16))
            images.append(jnp.concatenate(grads, axis=1))
        return jnp.concatenate(images, axis=0)

    for unit in units:
        emit(*unit, jnp.dot(grad_of(*unit, score_of(*unit)), everyone, preferred_element_type=F32))


def pixel_kernel(held, pixels, tracks, place, *refs):
    block_refs, (frames_ref, out_hbm, out, sems) = refs[:-4], refs[-4:]
    lane_tiles = C // LANES
    lines_out = held * lane_tiles
    own = out.shape[0] // lines_out
    copies = []

    def emit(first, t, value):
        chunk = value.shape[0]
        for k in range(lane_tiles):
            out[pl.ds(first * lines_out + k * held + t, chunk, stride=lines_out), :] = value[
                :, k * LANES : (k + 1) * LANES
            ]
        if t == held - 1:
            rows = pl.ds(first * lines_out, chunk * lines_out)
            copy = pltpu.make_async_copy(out.at[rows, :], out_hbm.at[rows, :], sems.at[first // chunk])
            copy.start()
            copies.append(copy)

    frame_kernel(held, pixels, own, tracks, place, block_refs, frames_ref, emit)
    for copy in copies:
        copy.wait()


def on_device(sizes, frames, query_frame, query_pixel, cotangent):
    return steps_on_device(sizes, frames, query_frame, query_pixel, cotangent)


def steps_on_device(sizes, frames, query_frame, query_pixel, cotangent):
    ranks, columns = sizes["frame"], sizes["track"]
    held, pixels, channels = frames.shape
    tracks = query_frame.shape[0]
    place = jnp.stack([lax.axis_index("frame"), lax.axis_index("track")]).astype(jnp.int32)
    frames_hbm, frame_hbm, pixel_hbm = (
        pltpu.with_memory_space_constraint(value, pltpu.HBM)
        for value in (frames.reshape(held * pixels, channels), query_frame[None], query_pixel[None])
    )

    kept, feat = pl.pallas_call(
        functools.partial(pick_kernel, held, pixels),
        out_shape=(pltpu.VMEM((held * pixels, channels), BF16), pltpu.VMEM((tracks, channels), BF16)),
        in_specs=[SMEM_SPEC, HBM_SPEC, HBM_SPEC, HBM_SPEC],
        out_specs=(VMEM_SPEC, VMEM_SPEC),
        scratch_shapes=[
            pltpu.VMEM((2, tracks), jnp.int32),
            pltpu.VMEM((2, tracks, channels), F32),
            pltpu.SemaphoreType.DMA((held * pixels // COPY_ROWS + 2,)),
        ],
        compiler_params=PARAMS,
        name="pick",
    )(place, frame_hbm, pixel_hbm, frames_hbm)

    picks = [feat]
    for i in range(1, ranks):
        picks.append(xor_permute(feat, "frame", ranks, i))
    flipped = pl.pallas_call(
        flip_kernel,
        out_shape=pltpu.VMEM((channels, held * pixels), BF16),
        in_specs=[VMEM_SPEC],
        out_specs=VMEM_SPEC,
        compiler_params=PARAMS,
        cost_estimate=pl.CostEstimate(flops=0, bytes_accessed=4 * held * pixels * channels, transcendentals=0),
        name="flip",
    )(kept)
    feat = sum(picks[1:], picks[0])

    share = tracks // ranks
    packed, *terms = pl.pallas_call(
        lambda place_ref, *refs: track_kernel(held, pixels, place_ref, ranks, *refs),
        out_shape=(pltpu.VMEM((tracks + stat_rows_of(held, tracks), channels), BF16),)
        + tuple(pltpu.VMEM((share, channels), F32) for _ in range(ranks)),
        in_specs=[SMEM_SPEC, VMEM_SPEC, VMEM_SPEC, VMEM_SPEC, VMEM_SPEC],
        out_specs=(VMEM_SPEC,) * (1 + ranks),
        scratch_shapes=[
            *[pltpu.VMEM((tracks, pixels), F32)] * held,
            pltpu.VMEM((2, tracks, channels), F32),
            pltpu.VMEM((held, tracks, LANES), F32),
        ]
        + [pltpu.VMEM((tracks, LANES), F32)] * 4,
        compiler_params=PARAMS,
        name="own_tracks",
    )(place, feat, kept, flipped, cotangent)

    far_blocks, distance = [], columns // 2
    while distance > 1:
        far_blocks += [xor_permute(block, "track", columns, distance) for block in [packed] + far_blocks]
        distance //= 2
    arrived = []
    for i in range(1, ranks):
        arrived.append(xor_permute(terms[i], "frame", ranks, i))
    near_blocks = [packed, xor_permute(packed, "track", columns, 1)]

    own = pixels // columns
    lines_out = held * channels // LANES

    def cost(count):
        return pl.CostEstimate(
            flops=4 * held * own * tracks * count * channels,
            bytes_accessed=4 * held * own * channels,
            transcendentals=held * own * tracks * count,
        )

    far_blocks += [xor_permute(block, "track", columns, 1) for block in far_blocks]
    query_grad = terms[0]

    frame_grad = pl.pallas_call(
        functools.partial(pixel_kernel, held, pixels, tracks),
        out_shape=jax.ShapeDtypeStruct((own * lines_out, LANES), F32),
        in_specs=[SMEM_SPEC] + [VMEM_SPEC] * (columns + 1),
        out_specs=HBM_SPEC,
        scratch_shapes=[
            pltpu.VMEM((own * lines_out, LANES), F32),
            pltpu.SemaphoreType.DMA((own // min(own, PIXEL_ROWS),)),
        ],
        compiler_params=PARAMS,
        cost_estimate=cost(columns),
        name="own_pixels",
    )(place, *near_blocks, *far_blocks, kept)
    frame_grad, query_grad, *arrived = lax.optimization_barrier((frame_grad, query_grad, *arrived))
    frame_grad = frame_grad.reshape(own, channels // LANES, held, LANES)
    frame_grad = jnp.transpose(frame_grad, (0, 2, 1, 3)).reshape(own, held, channels)
    for value in arrived:
        query_grad = query_grad + value
    return (frame_grad, query_grad)


def solution(mesh):
    return jax.shard_map(
        functools.partial(on_device, dict(mesh.shape)),
        mesh=mesh,
        in_specs=(
            P(("groups", "frame"), None, None),
            P(("groups", "track")),
            P(("groups", "track")),
            P(None, ("groups", "frame"), "track"),
        ),
        out_specs=(P("track", ("groups", "frame"), None), P(("groups", "track", "frame"), None)),
        check_vma=False,
    )
```
